512 devices in a mesh: seq: 64 (over y, x, core), head: 8 (over z).
Axes of the slice: x: 4, y: 8, z: 8, core: 2. Of those that a mesh axis runs over, the one named last changes fastest.
Arguments:
- queries: bfloat16 [16384, 4096], P('seq', 'head'), may hold values from -6 to 6
- key_rows: bfloat16 [16384, 4096], P('seq', 'head'), may hold values from -6 to 6
- values: bfloat16 [16384, 4096], P('seq', 'head'), may hold values from -12 to 12
- cotangent: bfloat16 [16384, 4096], P('seq', 'head'), may hold values from -12 to 12
- carried_state: float32 [32, 128, 128], P('head'), may hold values from -192 to 192
- norm_gain: float32 [4096], P('head'), may hold values from 0.25 to 1.75
Outputs:
- attended: bfloat16 [16384, 4096], P('seq', 'head')
- gradient_queries: bfloat16 [16384, 4096], P('seq', 'head')
- gradient_keys: bfloat16 [16384, 4096], P('seq', 'head')
- grad_value: bfloat16 [16384, 4096], P('seq', 'head')
- grad_state: float32 [32, 128, 128], P('head')
- grad_gain: float32 [4096], P('head')
The draws below stay inside these ranges and needn't reach their ends.
All inputs are finite; a program needn't handle non-finite values.
Results may differ from the reference program's by a relative error of at most 0.0065.
Values may be sent and summed in bfloat16 or wider, within the bound.
A program may use at most 64 MiB of HBM per device.

```python
import jax
import jax.numpy as jnp
from jax import lax

DH = 128
TOK_DEV = 256
HEADS = 32
F = 4096
TOKENS = 16384


def draw_values(key, part):
    columns = jnp.arange(HEADS * DH)
    position = (columns // DH).astype(jnp.float32) / max(HEADS - 1, 1)
    noise = jnp.clip(jax.random.normal(key, (TOKENS, HEADS * DH), jnp.float32), -6.0, 6.0)
    factor = 0.6 * jnp.power(3.0, position)
    return (noise * factor[None, :]).astype(jnp.bfloat16)


def draw_cotangent(key, part):
    first = jax.random.fold_in(key, 0)
    position = jnp.arange(TOKENS).astype(jnp.float32) / max(TOKENS - 1, 1)
    noise = jnp.clip(jax.random.normal(first, (TOKENS, HEADS * DH), jnp.float32), -6.0, 6.0)
    factor = 0.6 * jnp.power(3.0, position)
    result = noise * factor[:, None]
    return result.astype(jnp.bfloat16)


def shard_levels(own_key, shape, pieces, least, top_value):
    level = 1.0
    for dim, blocks in pieces:
        draws = jax.random.uniform(jax.random.fold_in(jax.random.fold_in(own_key, 6), dim), (blocks,), jnp.float32, least / len(pieces), top_value / len(pieces))
        level = level * jnp.repeat(jnp.exp(draws), shape[dim] // blocks).reshape((-1,) + (1,) * (len(shape) - 1 - dim))
    return level


def bell_draw(own_key, dims, scale, limit, cuts=(), held_as=jnp.bfloat16):
    drawn = jax.random.normal(own_key, dims, jnp.float32) * scale
    if len(cuts) > 0:
        drawn = shard_levels(own_key, dims, cuts, -0.22, 0.18) * drawn
    return jnp.clip(drawn, min=-limit, max=limit).astype(held_as)


def setup_inputs(seed: int = 0) -> dict:
    arg_keys = jax.random.split(jax.random.key(seed), 7)
    queries = bell_draw(arg_keys[0], (TOKENS, F), 1.0, 6.0, ((0, 64), (1, 8)))
    key_rows = bell_draw(arg_keys[1], (TOKENS, F), 1.0, 6.0, ((0, 64), (1, 8)))
    values = draw_values(jax.random.fold_in(arg_keys[6], 71), 0)
    cotangent = draw_cotangent(jax.random.fold_in(arg_keys[6], 71), 0)
    carried_state = bell_draw(arg_keys[4], (HEADS, DH, DH), (TOK_DEV // 8), 192.0, ((0, 8),), jnp.float32)
    norm_gain = jnp.clip(1.0 + 0.15 * jax.random.normal(arg_keys[5], (F,), jnp.float32), 0.25, 1.75)
    return dict(queries=queries, key_rows=key_rows, values=values, cotangent=cotangent, carried_state=carried_state, norm_gain=norm_gain)


EPS = 1e-05

def inner_product(form, left, right):
    return jnp.einsum(form, left.astype(jnp.float32), right.astype(jnp.float32), precision=lax.Precision.HIGHEST)

def reference(queries, key_rows, values, cotangent, carried_state, norm_gain):
    blocks = TOKENS // TOK_DEV
    width = HEADS * DH

    def split(rows):
        return rows.reshape(blocks, TOK_DEV, HEADS, DH)
    causal_mask = jnp.arange(TOK_DEV)[:, None] >= jnp.arange(TOK_DEV)[None, :]
    gain_heads = norm_gain.astype(jnp.float32).reshape(HEADS, DH)

    def forward_block(prefix, inputs):
        block_queries, block_keys, block_values, cot_b = inputs
        preceding_part = prefix.astype(jnp.bfloat16)
        score_matrix = jnp.where(causal_mask, inner_product('ftz,ytz->tfy', block_queries, block_keys), jnp.float32(0.0)).astype(jnp.bfloat16)
        unnormed = inner_product('hlm,mhe->lhe', score_matrix, block_values) + inner_product('lhd,hde->lhe', block_queries, preceding_part)
        square_sum = lax.optimization_barrier(jnp.sum(unnormed * unnormed, axis=(1, 2)))
        norm_scale = jnp.sqrt(square_sum / width + EPS)[:, None, None]
        normed = unnormed / norm_scale
        attended = (gain_heads * normed).astype(jnp.bfloat16)
        cot_wide = cot_b.astype(jnp.float32)
        scaled = cot_wide * gain_heads
        dot_sum = lax.optimization_barrier(jnp.sum(scaled * unnormed, axis=(1, 2)))[:, None, None]
        grad_unnormed = ((scaled - normed * (dot_sum / (width * norm_scale))) / norm_scale).astype(jnp.bfloat16)
        gain_term = lax.optimization_barrier(jnp.sum(cot_wide * normed, axis=0))
        grad_group = inner_product('lhd,lhe->hde', block_queries, grad_unnormed)
        group_state = inner_product('lhd,lhe->hde', block_keys, block_values)
        return (prefix + group_state, (prefix, attended, grad_unnormed, gain_term, grad_group))
    inputs = (split(queries), split(key_rows), split(values), split(cotangent))
    unused, outputs = lax.scan(forward_block, carried_state.astype(jnp.float32), inputs)
    prefixes, attended, grad_unnormed, gain_terms, grad_groups = outputs
    grad_state = lax.optimization_barrier(jnp.sum(grad_groups, axis=0))
    inclusive = lax.cumsum(grad_groups, axis=0, reverse=True)
    suffixes = jnp.concatenate([inclusive[1:], jnp.zeros_like(inclusive[:1])], axis=0)

    def backward_block(items):
        block_queries, block_keys, block_values, block_gradient, prefix, suffix = items
        preceding_part = prefix.astype(jnp.bfloat16)
        following_part = suffix.astype(jnp.bfloat16)
        score_matrix = jnp.where(causal_mask, inner_product('ftz,ytz->tfy', block_queries, block_keys), jnp.float32(0.0)).astype(jnp.bfloat16)
        blended_output = jnp.where(causal_mask, inner_product('lhe,mhe->hlm', block_gradient, block_values), jnp.float32(0.0)).astype(jnp.bfloat16)
        query_gradient = inner_product('krx,xkn->rkn', blended_output, block_keys) + inner_product('xif,iuf->xiu', block_gradient, preceding_part)
        key_gradient = inner_product('nox,ony->xny', blended_output, block_queries) + inner_product('yon,otn->yot', block_values, following_part)
        value_gradient = inner_product('nou,onk->unk', score_matrix, block_gradient) + inner_product('klj,ljr->klr', block_keys, following_part)
        return (query_gradient.astype(jnp.bfloat16), key_gradient.astype(jnp.bfloat16), value_gradient.astype(jnp.bfloat16))
    query_gradient, key_gradient, value_gradient = lax.map(backward_block, (inputs[0], inputs[1], inputs[2], grad_unnormed, prefixes, suffixes))
    grad_gain = lax.optimization_barrier(jnp.sum(gain_terms, axis=0)).reshape(width)
    return (attended.reshape(TOKENS, width), query_gradient.reshape(TOKENS, width), key_gradient.reshape(TOKENS, width), value_gradient.reshape(TOKENS, width), grad_state, grad_gain)
```

```python
import jax
import jax.numpy as jnp
from jax import lax
from jax.experimental import pallas as pl
from jax.experimental.pallas import tpu as pltpu
from jax.sharding import PartitionSpec as P

EPS = 1e-05
MESH = pl.DeviceIdType.MESH
F32 = jnp.float32
BF16 = jnp.bfloat16
ROW = 8
COL = 8
NZ = 8
HEADS = 4
D = 128
L = 256
WIDTH = HEADS * D
TOTAL_WIDTH = WIDTH * NZ
HALF = D // 2


def nn(a, b):
    return lax.dot_general(a, b, (((1,), (0,)), ((), ())), preferred_element_type=F32)


def nt(a, b):
    return lax.dot_general(a, b, (((1,), (1,)), ((), ())), preferred_element_type=F32)


def tn(a, b):
    return lax.dot_general(a, b, (((0,), (0,)), ((), ())), preferred_element_type=F32)


def comm_kernel(
    q_hbm, k_hbm, v_hbm, c_hbm, carry_hbm, gain_hbm,
    att_o, gq_o, gkp_o, gvp_o, suf_o, tot_o, gg_o,
    q, k, v, c, carry, gain,
    sb, rb, cb, ps, pre,
    sb2, rb2, cb2, ps2, suf, tot,
    zb, grow, gcol,
    sc_t, un, gu, att, gq, gkp, gvp, gg,
    in_sem, out_sem, send_sem, recv_sem,
):
    seq = lax.axis_index("seq")
    z = lax.axis_index("head")
    y = seq // ROW
    me = seq % ROW
    base = y * ROW

    def row_dev(kk):
        return (base + lax.rem(me + kk, ROW), z)

    def col_dev(kk):
        return (lax.rem(y + kk, COL) * ROW + me, z)

    def z_dev(kk):
        return (seq, lax.rem(z + kk, NZ))

    barrier = pltpu.get_barrier_semaphore()
    for dev, count in ((row_dev, ROW), (col_dev, COL), (z_dev, NZ)):
        for kk in range(1, count):
            pl.semaphore_signal(barrier, inc=1, device_id=dev(kk), device_id_type=MESH)

    loads = []
    for i, (src, dst) in enumerate(
        ((k_hbm, k), (v_hbm, v), (q_hbm, q), (c_hbm, c), (carry_hbm.at[me], carry), (gain_hbm, gain))
    ):
        load = pltpu.make_async_copy(src, dst, in_sem.at[i])
        load.start()
        loads.append(load)

    pending = []

    def exchange(stage, dev, count, src_of, dst, mine):
        copies = []
        for kk in range(1, count):
            target = lax.rem(mine + kk, count)
            copy = pltpu.make_async_remote_copy(
                src_ref=src_of(target),
                dst_ref=dst.at[mine],
                send_sem=send_sem.at[stage, kk],
                recv_sem=recv_sem.at[stage, kk],
                device_id=dev(kk),
                device_id_type=MESH,
            )
            copy.start()
            copies.append(copy)
        pending.extend(copies)

        def wait():
            for kk in range(1, count):
                origin = lax.rem(mine + count - kk, count)
                pltpu.make_async_remote_copy(
                    src_ref=src_of(origin),
                    dst_ref=dst.at[origin],
                    send_sem=send_sem.at[stage, kk],
                    recv_sem=recv_sem.at[stage, kk],
                    device_id=dev(kk),
                    device_id_type=MESH,
                ).wait_recv()

        return wait

    def head(ref, h):
        return ref[:, h * D:(h + 1) * D]

    rows = lax.broadcasted_iota(jnp.int32, (L, L), 0)
    cols = lax.broadcasted_iota(jnp.int32, (L, L), 1)
    lower = rows >= cols
    upper = rows <= cols

    loads[0].wait()
    loads[1].wait()
    for h in range(HEADS):
        state = tn(head(k, h), head(v, h)).astype(BF16)
        sb[2 * h] = state[:HALF]
        sb[2 * h + 1] = state[HALF:]
    pl.semaphore_wait(barrier, ROW + COL + NZ - 3)
    wait_a = exchange(0, row_dev, ROW, lambda t: sb.at[t], rb, me)
    rb[me] = sb[me]

    loads[2].wait()
    for h in range(HEADS):
        score = jnp.where(lower, nt(head(q, h), head(k, h)), 0.0).astype(BF16)
        un[h] = nn(score, head(v, h))

    wait_a()
    acc = rb[0].astype(F32)
    for r in range(1, ROW):
        acc = acc + rb[r].astype(F32)
    cb[y] = acc.astype(BF16)
    wait_b = exchange(1, col_dev, COL, lambda t: cb.at[y], cb, y)

    for h in range(HEADS):
        sc_t[h] = jnp.where(upper, nt(head(k, h), head(q, h)), 0.0).astype(BF16)
    loads[3].wait()
    loads[4].wait()
    loads[5].wait()

    wait_b()
    acc = carry[...]
    for r in range(COL):
        acc = acc + jnp.where(r < y, cb[r].astype(F32), 0.0)
    for r in range(ROW):
        ps[r] = acc.astype(BF16)
        if r < ROW - 1:
            acc = acc + rb[r].astype(F32)
    wait_c = exchange(2, row_dev, ROW, lambda t: ps.at[t], pre, me)
    pre[me] = ps[me]
    wait_c()

    square = jnp.zeros((L, D), F32)
    dots = jnp.zeros((L, D), F32)
    for h in range(HEADS):
        u = un[h] + nn(head(q, h), pre[2 * h:2 * h + 2].reshape(D, D))
        un[h] = u
        square = square + u * u
        dots = dots + head(c, h).astype(F32) * head(gain, h) * u

    def lane_sum(x):
        return jnp.sum(x.T, axis=0, keepdims=True)

    tile_row = lax.broadcasted_iota(jnp.int32, (8, D), 0)
    parts = (lane_sum(square[:D]), lane_sum(square[D:]), lane_sum(dots[:D]), lane_sum(dots[D:]))
    tile = jnp.zeros((8, D), F32)
    for i, part in enumerate(parts):
        tile = jnp.where(tile_row == i, part, tile)
    zb[z] = tile
    wait_z = exchange(3, z_dev, NZ, lambda t: zb.at[z], zb, z)
    wait_z()
    sums = zb[0]
    for i in range(1, NZ):
        sums = sums + zb[i]
    mean = sums[0:2] / TOTAL_WIDTH + EPS
    inverse = 1.0 / jnp.sqrt(mean)
    factor = sums[2:4] / (TOTAL_WIDTH * mean)
    both = jnp.concatenate([inverse, factor, jnp.zeros((4, D), F32)], axis=0).T
    inv_col = jnp.concatenate([both[:, 0:1], both[:, 1:2]], axis=0)
    fac_col = jnp.concatenate([both[:, 2:3], both[:, 3:4]], axis=0)
    inv_col = jnp.broadcast_to(inv_col, (L, D))
    fac_col = jnp.broadcast_to(fac_col, (L, D))

    grow[me] = jnp.zeros((8, D), F32)
    for h in range(HEADS):
        cot = head(c, h).astype(F32)
        g = ((cot * head(gain, h) - un[h] * fac_col) * inv_col).astype(BF16)
        gu[h] = g
        state = tn(head(q, h), g).astype(BF16)
        sb2[2 * h] = state[:HALF]
        sb2[2 * h + 1] = state[HALF:]
    wait_a = exchange(4, row_dev, ROW, lambda t: sb2.at[t], rb2, me)
    rb2[me] = sb2[me]

    for h in range(HEADS):
        normed = un[h] * inv_col
        att[:, h * D:(h + 1) * D] = (normed * head(gain, h)).astype(BF16)
        part = jnp.sum(head(c, h).astype(F32) * normed, axis=0, keepdims=True)
        grow[me, h:h + 1] = part
    wait_g = exchange(5, row_dev, ROW, lambda t: grow.at[me], grow, me)
    out_att = pltpu.make_async_copy(att, att_o, out_sem.at[0])
    out_att.start()

    for h in range(HEADS):
        mixed = jnp.where(lower, nt(gu[h], head(v, h)), 0.0).astype(BF16)
        gq[:, h * D:(h + 1) * D] = (
            nn(mixed, head(k, h)) + nt(gu[h], pre[2 * h:2 * h + 2].reshape(D, D))
        ).astype(BF16)
    out_gq = pltpu.make_async_copy(gq, gq_o, out_sem.at[1])
    out_gq.start()

    wait_a()
    acc = rb2[0].astype(F32)
    for r in range(1, ROW):
        acc = acc + rb2[r].astype(F32)
    cb2[y] = acc.astype(BF16)
    wait_b = exchange(6, col_dev, COL, lambda t: cb2.at[y], cb2, y)
    wait_g()
    gsum = grow[0]
    for r in range(1, ROW):
        gsum = gsum + grow[r]
    gcol[y] = gsum
    wait_g = exchange(7, col_dev, COL, lambda t: gcol.at[y], gcol, y)

    for h in range(HEADS):
        mixed_t = jnp.where(upper, nt(head(v, h), gu[h]), 0.0).astype(BF16)
        gkp[:, h * D:(h + 1) * D] = nn(mixed_t, head(q, h))
        gvp[:, h * D:(h + 1) * D] = nn(sc_t[h], gu[h])
    out_gk = pltpu.make_async_copy(gkp, gkp_o, out_sem.at[2])
    out_gk.start()
    out_gv = pltpu.make_async_copy(gvp, gvp_o, out_sem.at[3])
    out_gv.start()

    wait_b()
    total = cb2[0].astype(F32)
    acc = jnp.zeros((HALF, D), F32)
    for r in range(COL):
        part = cb2[r].astype(F32)
        if r:
            total = total + part
        acc = acc + jnp.where(r > y, part, 0.0)
    for r in range(ROW - 1, -1, -1):
        ps2[r] = acc.astype(BF16)
        if r:
            acc = acc + rb2[r].astype(F32)
    wait_c = exchange(8, row_dev, ROW, lambda t: ps2.at[t], suf, me)
    tot[me] = total.astype(BF16)
    wait_t = exchange(9, row_dev, ROW, lambda t: tot.at[me], tot, me)
    suf[me] = ps2[me]
    wait_g()
    gsum = gcol[0]
    for r in range(1, COL):
        gsum = gsum + gcol[r]
    gg[...] = gsum
    out_gg = pltpu.make_async_copy(gg, gg_o, out_sem.at[4])
    out_gg.start()
    wait_c()
    out_suf = pltpu.make_async_copy(suf, suf_o, out_sem.at[5])
    out_suf.start()
    wait_t()
    out_tot = pltpu.make_async_copy(tot, tot_o, out_sem.at[6])
    out_tot.start()
    for copy in pending:
        copy.wait_send()
    for copy in (out_att, out_gq, out_gk, out_gv, out_gg, out_suf, out_tot):
        copy.wait()


def tail_kernel(k, v, att_i, gq_i, gkp, gvp, suf, tot, gg, att, gq, gk, gv, gs, gain):
    att[...] = att_i[...]
    gq[...] = gq_i[...]
    for h in range(HEADS):
        lanes = slice(h * D, (h + 1) * D)
        suffix = suf[2 * h:2 * h + 2].reshape(D, D)
        gk[:, lanes] = (gkp[:, lanes] + nt(v[:, lanes], suffix)).astype(BF16)
        gv[:, lanes] = (gvp[:, lanes] + nn(k[:, lanes], suffix)).astype(BF16)
        gain[:, lanes] = gg[h:h + 1]
    gs[...] = tot[...].astype(F32)


def on_device(queries, key_rows, values, cotangent, carried_state, norm_gain):
    any_spec = pl.BlockSpec(memory_space=pl.ANY)
    vmem_spec = pl.BlockSpec(memory_space=pltpu.VMEM)
    wide = (L, WIDTH)
    slices = (ROW, HALF, D)
    sds = jax.ShapeDtypeStruct
    att, gq, gkp, gvp, suf, tot, gg = pl.pallas_call(
        comm_kernel,
        out_shape=(
            sds(wide, BF16), sds(wide, BF16), sds(wide, F32), sds(wide, F32),
            sds(slices, BF16), sds(slices, BF16), sds((8, D), F32),
        ),
        in_specs=[any_spec] * 6,
        out_specs=[any_spec] * 7,
        scratch_shapes=[
            pltpu.VMEM(wide, BF16), pltpu.VMEM(wide, BF16), pltpu.VMEM(wide, BF16), pltpu.VMEM(wide, BF16),
            pltpu.VMEM((HALF, D), F32), pltpu.VMEM((1, WIDTH), F32),
            *[pltpu.VMEM(slices, BF16)] * 5,
            *[pltpu.VMEM(slices, BF16)] * 6,
            pltpu.VMEM((NZ, 8, D), F32), pltpu.VMEM((ROW, 8, D), F32), pltpu.VMEM((COL, 8, D), F32),
            pltpu.VMEM((HEADS, L, L), BF16), pltpu.VMEM((HEADS, L, D), F32), pltpu.VMEM((HEADS, L, D), BF16),
            pltpu.VMEM(wide, BF16), pltpu.VMEM(wide, BF16), pltpu.VMEM(wide, F32), pltpu.VMEM(wide, F32),
            pltpu.VMEM((8, D), F32),
            pltpu.SemaphoreType.DMA((6,)), pltpu.SemaphoreType.DMA((7,)),
            pltpu.SemaphoreType.DMA((10, 8)), pltpu.SemaphoreType.DMA((10, 8)),
        ],
        compiler_params=pltpu.CompilerParams(collective_id=0, has_side_effects=True),
        name="scan_comm",
    )(queries, key_rows, values, cotangent, carried_state.reshape(slices), norm_gain.reshape(1, WIDTH))
    att, gq, gk, gv, gs, gain = pl.pallas_call(
        tail_kernel,
        out_shape=(
            sds(wide, BF16), sds(wide, BF16), sds(wide, BF16), sds(wide, BF16),
            sds(slices, F32), sds((1, WIDTH), F32),
        ),
        in_specs=[vmem_spec] * 9,
        out_specs=[vmem_spec] * 6,
        name="tail",
    )(key_rows, values, att, gq, gkp, gvp, suf, tot, gg)
    return att, gq, gk, gv, gs.reshape(HEADS, D, D), gain.reshape(WIDTH)


def solution(mesh):
    in_specs = (
        P("seq", "head"),
        P("seq", "head"),
        P("seq", "head"),
        P("seq", "head"),
        P("head", None, None),
        P("head"),
    )
    out_specs = (
        P("seq", "head"),
        P("seq", "head"),
        P("seq", "head"),
        P("seq", "head"),
        P("head", None, None),
        P("head"),
    )
    return jax.shard_map(
        on_device, mesh=mesh, in_specs=in_specs, out_specs=out_specs, check_vma=False
    )
```

```python
import jax
import jax.numpy as jnp
from jax import lax
from jax.experimental import pallas as pl
from jax.experimental.pallas import tpu as pltpu
from jax.sharding import PartitionSpec as P

EPS = 1e-05
MESH = pl.DeviceIdType.MESH
F32 = jnp.float32
BF16 = jnp.bfloat16
ROW = 8
COL = 8
NZ = 8
HEADS = 4
D = 128
L = 256
WIDTH = HEADS * D
TOTAL_WIDTH = WIDTH * NZ
HALF = D // 2
CHUNKS = 1
PIECE = HALF // CHUNKS
FAR_FIRST = (4, 3, 5, 2, 6, 1, 7)


def nn(a, b):
    return lax.dot_general(a, b, (((1,), (0,)), ((), ())), preferred_element_type=F32)


def nt(a, b):
    return lax.dot_general(a, b, (((1,), (1,)), ((), ())), preferred_element_type=F32)


def tn(a, b):
    return lax.dot_general(a, b, (((0,), (0,)), ((), ())), preferred_element_type=F32)


def comm_kernel(
    q_hbm, k_hbm, v_hbm, c_hbm, carry_hbm, gain_hbm,
    k, v, att, gq, gkp, gvp, suf, tot, gg,
    q, c, carry, gain,
    sb, rb, cb, ps, pre,
    sb2, rb2, cb2, ps2,
    zb, grow, gcol,
    sc_t, un, gu,
    in_sem, send_sem, recv_sem, tile_send, tile_recv,
):
    seq = lax.axis_index("seq")
    z = lax.axis_index("head")
    y = seq // ROW
    me = seq % ROW
    base = y * ROW

    def row_dev(kk):
        return (base + lax.rem(me + kk, ROW), z)

    def col_dev(kk):
        return (lax.rem(y + kk, COL) * ROW + me, z)

    def z_dev(kk):
        return (seq, lax.rem(z + kk, NZ))

    barrier = pltpu.get_barrier_semaphore()
    for dev, count in ((row_dev, ROW), (col_dev, COL), (z_dev, NZ)):
        for kk in range(1, count):
            pl.semaphore_signal(barrier, inc=1, device_id=dev(kk), device_id_type=MESH)

    loads = []
    for i, (src, dst) in enumerate(
        ((k_hbm, k), (v_hbm, v), (q_hbm, q), (c_hbm, c), (carry_hbm.at[me], carry), (gain_hbm, gain))
    ):
        load = pltpu.make_async_copy(src, dst, in_sem.at[i])
        load.start()
        loads.append(load)

    pending = []

    def exchange(sends, recvs, dev, count, src_of, dst_of, mine):
        for kk in FAR_FIRST:
            copy = pltpu.make_async_remote_copy(
                src_ref=src_of(lax.rem(mine + kk, count)),
                dst_ref=dst_of(mine),
                send_sem=sends.at[kk],
                recv_sem=recvs.at[kk],
                device_id=dev(kk),
                device_id_type=MESH,
            )
            copy.start()
            pending.append(copy)

        def wait():
            for kk in FAR_FIRST[::-1]:
                origin = lax.rem(mine + count - kk, count)
                pltpu.make_async_remote_copy(
                    src_ref=src_of(origin),
                    dst_ref=dst_of(origin),
                    send_sem=sends.at[kk],
                    recv_sem=recvs.at[kk],
                    device_id=dev(kk),
                    device_id_type=MESH,
                ).wait_recv()

        return wait

    def strip(n):
        return slice(n * PIECE, (n + 1) * PIECE)

    def piece(ref, i, n):
        return ref.at[i, pl.ds(n * PIECE, PIECE)]

    def scatter(stage, n, dev, count, src, dst, mine):
        return exchange(
            send_sem.at[stage, n], recv_sem.at[stage, n], dev, count,
            lambda t: piece(src, t, n), lambda t: piece(dst, t, n), mine,
        )

    def spread(stage, n, dev, count, ref, mine):
        return exchange(
            send_sem.at[stage, n], recv_sem.at[stage, n], dev, count,
            lambda t: piece(ref, mine, n), lambda t: piece(ref, t, n), mine,
        )

    def tiles(stage, dev, count, ref, mine):
        return exchange(
            tile_send.at[stage], tile_recv.at[stage], dev, count,
            lambda t: ref.at[mine], lambda t: ref.at[t], mine,
        )

    def head(ref, h):
        return ref[:, h * D:(h + 1) * D]

    rows = lax.broadcasted_iota(jnp.int32, (L, L), 0)
    cols = lax.broadcasted_iota(jnp.int32, (L, L), 1)
    lower = rows >= cols
    upper = rows <= cols

    loads[0].wait()
    loads[1].wait()
    for h in range(HEADS):
        state = tn(head(k, h), head(v, h)).astype(BF16)
        sb[2 * h] = state[:HALF]
        sb[2 * h + 1] = state[HALF:]
    pl.semaphore_wait(barrier, ROW + COL + NZ - 3)
    waits_a = [scatter(0, n, row_dev, ROW, sb, rb, me) for n in range(CHUNKS)]
    rb[me] = sb[me]

    loads[2].wait()
    for h in range(HEADS):
        score = jnp.where(lower, nt(head(q, h), head(k, h)), 0.0).astype(BF16)
        un[h] = nn(score, head(v, h))

    waits_b = []
    for n in range(CHUNKS):
        waits_a[n]()
        acc = rb[0, strip(n)].astype(F32)
        for r in range(1, ROW):
            acc = acc + rb[r, strip(n)].astype(F32)
        cb[y, strip(n)] = acc.astype(BF16)
        waits_b.append(spread(1, n, col_dev, COL, cb, y))

    for h in range(HEADS):
        sc_t[h] = jnp.where(upper, nt(head(k, h), head(q, h)), 0.0).astype(BF16)
    loads[3].wait()
    loads[4].wait()
    loads[5].wait()

    waits_c = []
    for n in range(CHUNKS):
        waits_b[n]()
        acc = carry[strip(n)]
        for r in range(COL):
            acc = acc + jnp.where(r < y, cb[r, strip(n)].astype(F32), 0.0)
        for r in range(ROW):
            ps[r, strip(n)] = acc.astype(BF16)
            if r < ROW - 1:
                acc = acc + rb[r, strip(n)].astype(F32)
        waits_c.append(scatter(2, n, row_dev, ROW, ps, pre, me))
    pre[me] = ps[me]
    for wait in waits_c:
        wait()

    square = jnp.zeros((L, D), F32)
    dots = jnp.zeros((L, D), F32)
    for h in range(HEADS):
        u = un[h] + nn(head(q, h), pre[2 * h:2 * h + 2].reshape(D, D))
        un[h] = u
        square = square + u * u
        dots = dots + head(c, h).astype(F32) * head(gain, h) * u

    def lane_sum(x):
        return jnp.sum(x.T, axis=0, keepdims=True)

    tile_row = lax.broadcasted_iota(jnp.int32, (8, D), 0)
    parts = (lane_sum(square[:D]), lane_sum(square[D:]), lane_sum(dots[:D]), lane_sum(dots[D:]))
    tile = jnp.zeros((8, D), F32)
    for i, part in enumerate(parts):
        tile = jnp.where(tile_row == i, part, tile)
    zb[z] = tile
    tiles(0, z_dev, NZ, zb, z)()
    sums = zb[0]
    for i in range(1, NZ):
        sums = sums + zb[i]
    mean = sums[0:2] / TOTAL_WIDTH + EPS
    inverse = 1.0 / jnp.sqrt(mean)
    factor = sums[2:4] / (TOTAL_WIDTH * mean)
    both = jnp.concatenate([inverse, factor, jnp.zeros((4, D), F32)], axis=0).T
    inv_col = jnp.concatenate([both[:, 0:1], both[:, 1:2]], axis=0)
    fac_col = jnp.concatenate([both[:, 2:3], both[:, 3:4]], axis=0)
    inv_col = jnp.broadcast_to(inv_col, (L, D))
    fac_col = jnp.broadcast_to(fac_col, (L, D))

    grow[me] = jnp.zeros((8, D), F32)
    for h in range(HEADS):
        cot = head(c, h).astype(F32)
        g = ((cot * head(gain, h) - un[h] * fac_col) * inv_col).astype(BF16)
        gu[h] = g
        state = tn(head(q, h), g).astype(BF16)
        sb2[2 * h] = state[:HALF]
        sb2[2 * h + 1] = state[HALF:]
    waits_a = [scatter(3, n, row_dev, ROW, sb2, rb2, me) for n in range(CHUNKS)]
    rb2[me] = sb2[me]

    for h in range(HEADS):
        normed = un[h] * inv_col
        att[:, h * D:(h + 1) * D] = (normed * head(gain, h)).astype(BF16)
        grow[me, h:h + 1] = jnp.sum(head(c, h).astype(F32) * normed, axis=0, keepdims=True)
    wait_g = tiles(1, row_dev, ROW, grow, me)

    waits_b = []
    for n in range(CHUNKS):
        waits_a[n]()
        acc = rb2[0, strip(n)].astype(F32)
        for r in range(1, ROW):
            acc = acc + rb2[r, strip(n)].astype(F32)
        cb2[y, strip(n)] = acc.astype(BF16)
        waits_b.append(spread(4, n, col_dev, COL, cb2, y))
    wait_g()
    gsum = grow[0]
    for r in range(1, ROW):
        gsum = gsum + grow[r]
    gcol[y] = gsum
    wait_g = tiles(2, col_dev, COL, gcol, y)

    for h in range(HEADS):
        lanes = slice(h * D, (h + 1) * D)
        mixed = jnp.where(lower, nt(gu[h], head(v, h)), 0.0).astype(BF16)
        gq[:, lanes] = (
            nn(mixed, head(k, h)) + nt(gu[h], pre[2 * h:2 * h + 2].reshape(D, D))
        ).astype(BF16)
        mixed_t = jnp.where(upper, nt(head(v, h), gu[h]), 0.0).astype(BF16)
        gkp[:, lanes] = nn(mixed_t, head(q, h))
        gvp[:, lanes] = nn(sc_t[h], gu[h])

    waits_c = []
    waits_t = []
    for n in range(CHUNKS):
        waits_b[n]()
        total = cb2[0, strip(n)].astype(F32)
        acc = jnp.zeros((PIECE, D), F32)
        for r in range(COL):
            row_sum = cb2[r, strip(n)].astype(F32)
            if r:
                total = total + row_sum
            acc = acc + jnp.where(r > y, row_sum, 0.0)
        for r in range(ROW - 1, -1, -1):
            ps2[r, strip(n)] = acc.astype(BF16)
            if r:
                acc = acc + rb2[r, strip(n)].astype(F32)
        waits_c.append(scatter(5, n, row_dev, ROW, ps2, suf, me))
        tot[me, strip(n)] = total.astype(BF16)
        waits_t.append(spread(6, n, row_dev, ROW, tot, me))
    suf[me] = ps2[me]
    wait_g()
    gsum = gcol[0]
    for r in range(1, COL):
        gsum = gsum + gcol[r]
    gg[...] = gsum
    for wait in waits_c + waits_t:
        wait()
    for copy in pending:
        copy.wait_send()


def tail_kernel(
    k, v, att, gq, gkp, gvp, suf, tot, gg,
    att_o, gq_o, gk_o, gv_o, gs_o, gain_o,
    gk, gv, gs, gain, sem,
):
    copies = []

    def store(src, dst):
        copy = pltpu.make_async_copy(src, dst, sem.at[len(copies)])
        copy.start()
        copies.append(copy)

    store(att, att_o)
    store(gq, gq_o)
    for h in range(HEADS):
        lanes = slice(h * D, (h + 1) * D)
        gk[:, lanes] = (gkp[:, lanes] + nt(v[:, lanes], suf[2 * h:2 * h + 2].reshape(D, D))).astype(BF16)
    store(gk, gk_o)
    for h in range(HEADS):
        lanes = slice(h * D, (h + 1) * D)
        gv[:, lanes] = (gvp[:, lanes] + nn(k[:, lanes], suf[2 * h:2 * h + 2].reshape(D, D))).astype(BF16)
    store(gv, gv_o)
    gs[...] = tot[...].astype(F32)
    store(gs, gs_o)
    for h in range(HEADS):
        gain[:, h * D:(h + 1) * D] = gg[h:h + 1]
    store(gain, gain_o)
    for copy in copies:
        copy.wait()


def on_device(queries, key_rows, values, cotangent, carried_state, norm_gain):
    any_spec = pl.BlockSpec(memory_space=pl.ANY)
    vmem_spec = pl.BlockSpec(memory_space=pltpu.VMEM)
    wide = (L, WIDTH)
    slices = (ROW, HALF, D)
    sds = jax.ShapeDtypeStruct
    vmem = pltpu.VMEM
    held = (
        vmem(wide, BF16), vmem(wide, BF16), vmem(wide, BF16), vmem(wide, BF16),
        vmem(wide, F32), vmem(wide, F32), vmem(slices, BF16), vmem(slices, BF16), vmem((8, D), F32),
    )
    parts = pl.pallas_call(
        comm_kernel,
        out_shape=held,
        in_specs=[pl.BlockSpec(memory_space=pltpu.HBM)] * 6,
        out_specs=[vmem_spec] * 9,
        scratch_shapes=[
            vmem(wide, BF16), vmem(wide, BF16), vmem((HALF, D), F32), vmem((1, WIDTH), F32),
            *[vmem(slices, BF16)] * 5,
            *[vmem(slices, BF16)] * 4,
            vmem((NZ, 8, D), F32), vmem((ROW, 8, D), F32), vmem((COL, 8, D), F32),
            vmem((HEADS, L, L), BF16), vmem((HEADS, L, D), F32), vmem((HEADS, L, D), BF16),
            pltpu.SemaphoreType.DMA((6,)),
            pltpu.SemaphoreType.DMA((7, CHUNKS, 8)), pltpu.SemaphoreType.DMA((7, CHUNKS, 8)),
            pltpu.SemaphoreType.DMA((3, 8)), pltpu.SemaphoreType.DMA((3, 8)),
        ],
        compiler_params=pltpu.CompilerParams(
            collective_id=0, has_side_effects=True, vmem_limit_bytes=16 * 2**20
        ),
        name="scan_comm",
    )(*[pltpu.with_memory_space_constraint(x, pltpu.HBM) for x in (queries, key_rows, values, cotangent, carried_state.reshape(slices), norm_gain.reshape(1, WIDTH))])
    att, gq, gk, gv, gs, gain = pl.pallas_call(
        tail_kernel,
        out_shape=(
            sds(wide, BF16), sds(wide, BF16), sds(wide, BF16), sds(wide, BF16),
            sds(slices, F32), sds((1, WIDTH), F32),
        ),
        in_specs=[vmem_spec] * 9,
        out_specs=[any_spec] * 6,
        scratch_shapes=[
            vmem(wide, BF16), vmem(wide, BF16), vmem(slices, F32), vmem((1, WIDTH), F32),
            pltpu.SemaphoreType.DMA((6,)),
        ],
        compiler_params=pltpu.CompilerParams(vmem_limit_bytes=16 * 2**20),
        name="tail",
    )(*parts)
    return att, gq, gk, gv, gs.reshape(HEADS, D, D), gain.reshape(WIDTH)


def solution(mesh):
    in_specs = (
        P("seq", "head"),
        P("seq", "head"),
        P("seq", "head"),
        P("seq", "head"),
        P("head", None, None),
        P("head"),
    )
    out_specs = (
        P("seq", "head"),
        P("seq", "head"),
        P("seq", "head"),
        P("seq", "head"),
        P("head", None, None),
        P("head"),
    )
    return jax.shard_map(
        on_device, mesh=mesh, in_specs=in_specs, out_specs=out_specs, check_vma=False
    )
```

```python
import jax
import jax.numpy as jnp
from jax import lax
from jax.experimental import pallas as pl
from jax.experimental.pallas import tpu as pltpu
from jax.sharding import PartitionSpec as P

EPS = 1e-05
MESH = pl.DeviceIdType.MESH
F32 = jnp.float32
BF16 = jnp.bfloat16
ROW = 8
COL = 8
NZ = 8
HEADS = 4
D = 128
L = 256
WIDTH = HEADS * D
TOTAL_WIDTH = WIDTH * NZ
HALF = D // 2
TILE = 4
CHUNKS = 1
PIECE = HALF // CHUNKS
FAR_FIRST = (4, 3, 5, 2, 6, 1, 7)


def nn(a, b):
    return lax.dot_general(a, b, (((1,), (0,)), ((), ())), preferred_element_type=F32)


def nt(a, b):
    return lax.dot_general(a, b, (((1,), (1,)), ((), ())), preferred_element_type=F32)


def tn(a, b):
    return lax.dot_general(a, b, (((0,), (0,)), ((), ())), preferred_element_type=F32)


def comm_kernel(
    q_hbm, k_hbm, v_hbm, c_hbm, carry_hbm, gain_hbm,
    att, gq, gk, gv, tot, gg,
    q, k, v, c, carry, gain,
    sb, rb, cb, ps, pre,
    sb2, rb2, cb2, ps2, suf,
    zb, grow, gcol,
    sc_t, un, gu, gkp, gvp,
    in_sem, send_sem, recv_sem, tile_send, tile_recv,
):
    seq = lax.axis_index("seq")
    z = lax.axis_index("head")
    y = seq // ROW
    me = seq % ROW
    base = y * ROW

    def row_dev(kk):
        return (base + lax.rem(me + kk, ROW), z)

    def col_dev(kk):
        return (lax.rem(y + kk, COL) * ROW + me, z)

    def z_dev(kk):
        return (seq, lax.rem(z + kk, NZ))

    loads = []
    for i, (src, dst) in enumerate(
        ((k_hbm, k), (v_hbm, v), (q_hbm, q), (c_hbm, c), (carry_hbm.at[me], carry), (gain_hbm, gain))
    ):
        load = pltpu.make_async_copy(src, dst, in_sem.at[i])
        load.start()
        loads.append(load)

    barrier = pltpu.get_barrier_semaphore()
    for dev, count in ((row_dev, ROW), (col_dev, COL), (z_dev, NZ)):
        for kk in range(1, count):
            pl.semaphore_signal(barrier, inc=1, device_id=dev(kk), device_id_type=MESH)

    pending = []

    def exchange(sends, recvs, dev, count, src_of, dst_of, mine):
        for kk in FAR_FIRST:
            copy = pltpu.make_async_remote_copy(
                src_ref=src_of(lax.rem(mine + kk, count)),
                dst_ref=dst_of(mine),
                send_sem=sends.at[kk],
                recv_sem=recvs.at[kk],
                device_id=dev(kk),
                device_id_type=MESH,
            )
            copy.start()
            pending.append(copy)

        def wait():
            for kk in FAR_FIRST[::-1]:
                origin = lax.rem(mine + count - kk, count)
                pltpu.make_async_remote_copy(
                    src_ref=src_of(origin),
                    dst_ref=dst_of(origin),
                    send_sem=sends.at[kk],
                    recv_sem=recvs.at[kk],
                    device_id=dev(kk),
                    device_id_type=MESH,
                ).wait_recv()

        return wait

    def strip(n):
        return slice(n * PIECE, (n + 1) * PIECE)

    def piece(ref, i, n):
        return ref.at[i, pl.ds(n * PIECE, PIECE)]

    def scatter(stage, n, dev, count, src, dst, mine):
        return exchange(
            send_sem.at[stage, n], recv_sem.at[stage, n], dev, count,
            lambda t: piece(src, t, n), lambda t: piece(dst, t, n), mine,
        )

    def spread(stage, n, dev, count, ref, mine):
        return exchange(
            send_sem.at[stage, n], recv_sem.at[stage, n], dev, count,
            lambda t: piece(ref, mine, n), lambda t: piece(ref, t, n), mine,
        )

    def tiles(stage, dev, count, ref, mine):
        return exchange(
            tile_send.at[stage], tile_recv.at[stage], dev, count,
            lambda t: ref.at[mine], lambda t: ref.at[t], mine,
        )

    def head(ref, h):
        return ref[:, h * D:(h + 1) * D]

    rows = lax.broadcasted_iota(jnp.int32, (L, L), 0)
    cols = lax.broadcasted_iota(jnp.int32, (L, L), 1)
    lower = rows >= cols
    upper = rows <= cols

    loads[0].wait()
    loads[1].wait()
    for h in range(HEADS):
        state = tn(head(k, h), head(v, h)).astype(BF16)
        sb[2 * h] = state[:HALF]
        sb[2 * h + 1] = state[HALF:]
    pl.semaphore_wait(barrier, ROW + COL + NZ - 3)
    waits_a = [scatter(0, n, row_dev, ROW, sb, rb, me) for n in range(CHUNKS)]
    rb[me] = sb[me]

    loads[2].wait()
    for h in range(HEADS):
        score = jnp.where(lower, nt(head(q, h), head(k, h)), 0.0).astype(BF16)
        un[h] = nn(score, head(v, h))

    waits_b = []
    for n in range(CHUNKS):
        waits_a[n]()
        acc = rb[0, strip(n)].astype(F32)
        for r in range(1, ROW):
            acc = acc + rb[r, strip(n)].astype(F32)
        cb[y, strip(n)] = acc.astype(BF16)
        waits_b.append(spread(1, n, col_dev, COL, cb, y))

    for h in range(HEADS):
        sc_t[h] = jnp.where(upper, nt(head(k, h), head(q, h)), 0.0).astype(BF16)
    loads[3].wait()
    loads[4].wait()
    loads[5].wait()

    waits_c = []
    for n in range(CHUNKS):
        waits_b[n]()
        acc = carry[strip(n)]
        for r in range(COL):
            acc = acc + jnp.where(r < y, cb[r, strip(n)].astype(F32), 0.0)
        for r in range(ROW):
            ps[r, strip(n)] = acc.astype(BF16)
            if r < ROW - 1:
                acc = acc + rb[r, strip(n)].astype(F32)
        waits_c.append(scatter(2, n, row_dev, ROW, ps, pre, me))
    pre[me] = ps[me]
    for wait in waits_c:
        wait()

    square = jnp.zeros((L, D), F32)
    dots = jnp.zeros((L, D), F32)
    for h in range(HEADS):
        u = un[h] + nn(head(q, h), pre[2 * h:2 * h + 2].reshape(D, D))
        un[h] = u
        square = square + u * u
        dots = dots + head(c, h).astype(F32) * head(gain, h) * u

    def lane_sum(x):
        return jnp.sum(x.T, axis=0, keepdims=True)

    tile_row = lax.broadcasted_iota(jnp.int32, (TILE, D), 0)
    parts = (lane_sum(square[:D]), lane_sum(square[D:]), lane_sum(dots[:D]), lane_sum(dots[D:]))
    tile = jnp.zeros((TILE, D), F32)
    for i, part in enumerate(parts):
        tile = jnp.where(tile_row == i, part, tile)
    zb[z] = tile
    tiles(0, z_dev, NZ, zb, z)()
    sums = zb[0]
    for i in range(1, NZ):
        sums = sums + zb[i]
    mean = sums[0:2] / TOTAL_WIDTH + EPS
    inverse = 1.0 / jnp.sqrt(mean)
    factor = sums[2:4] / (TOTAL_WIDTH * mean)
    both = jnp.concatenate([inverse, factor, jnp.zeros((4, D), F32)], axis=0).T
    inv_col = jnp.concatenate([both[:, 0:1], both[:, 1:2]], axis=0)
    fac_col = jnp.concatenate([both[:, 2:3], both[:, 3:4]], axis=0)
    inv_col = jnp.broadcast_to(inv_col, (L, D))
    fac_col = jnp.broadcast_to(fac_col, (L, D))

    grow[me] = jnp.zeros((TILE, D), F32)
    for h in range(HEADS):
        cot = head(c, h).astype(F32)
        g = ((cot * head(gain, h) - un[h] * fac_col) * inv_col).astype(BF16)
        gu[h] = g
        state = tn(head(q, h), g).astype(BF16)
        sb2[2 * h] = state[:HALF]
        sb2[2 * h + 1] = state[HALF:]
    waits_a = [scatter(3, n, row_dev, ROW, sb2, rb2, me) for n in range(CHUNKS)]
    rb2[me] = sb2[me]

    for h in range(HEADS):
        normed = un[h] * inv_col
        att[:, h * D:(h + 1) * D] = (normed * head(gain, h)).astype(BF16)
        grow[me, h:h + 1] = jnp.sum(head(c, h).astype(F32) * normed, axis=0, keepdims=True)
    wait_g = tiles(1, row_dev, ROW, grow, me)

    waits_b = []
    for n in range(CHUNKS):
        waits_a[n]()
        acc = rb2[0, strip(n)].astype(F32)
        for r in range(1, ROW):
            acc = acc + rb2[r, strip(n)].astype(F32)
        cb2[y, strip(n)] = acc.astype(BF16)
        waits_b.append(spread(4, n, col_dev, COL, cb2, y))
    wait_g()
    gsum = grow[0]
    for r in range(1, ROW):
        gsum = gsum + grow[r]
    gcol[y] = gsum
    wait_g = tiles(2, col_dev, COL, gcol, y)

    for h in range(HEADS):
        lanes = slice(h * D, (h + 1) * D)
        mixed = jnp.where(lower, nt(gu[h], head(v, h)), 0.0).astype(BF16)
        gq[:, lanes] = (
            nn(mixed, head(k, h)) + nt(gu[h], pre[2 * h:2 * h + 2].reshape(D, D))
        ).astype(BF16)
        mixed_t = jnp.where(upper, nt(head(v, h), gu[h]), 0.0).astype(BF16)
        gkp[:, lanes] = nn(mixed_t, head(q, h))
        gvp[:, lanes] = nn(sc_t[h], gu[h])

    waits_c = []
    waits_t = []
    for n in range(CHUNKS):
        waits_b[n]()
        total = cb2[0, strip(n)].astype(F32)
        acc = jnp.zeros((PIECE, D), F32)
        for r in range(COL):
            row_sum = cb2[r, strip(n)].astype(F32)
            if r:
                total = total + row_sum
            acc = acc + jnp.where(r > y, row_sum, 0.0)
        for r in range(ROW - 1, -1, -1):
            ps2[r, strip(n)] = acc.astype(BF16)
            if r:
                acc = acc + rb2[r, strip(n)].astype(F32)
        waits_c.append(scatter(5, n, row_dev, ROW, ps2, suf, me))
        tot[me, strip(n)] = total.astype(BF16)
        waits_t.append(spread(6, n, row_dev, ROW, tot, me))
    suf[me] = ps2[me]
    wait_g()
    gsum = gcol[0]
    for r in range(1, COL):
        gsum = gsum + gcol[r]
    gg[...] = gsum
    for wait in waits_c:
        wait()
    for h in range(HEADS):
        lanes = slice(h * D, (h + 1) * D)
        suffix = suf[2 * h:2 * h + 2].reshape(D, D)
        gk[:, lanes] = (gkp[:, lanes] + nt(head(v, h), suffix)).astype(BF16)
        gv[:, lanes] = (gvp[:, lanes] + nn(head(k, h), suffix)).astype(BF16)
    for wait in waits_t:
        wait()
    for copy in pending:
        copy.wait_send()


def tail_kernel(
    att, gq, gk, gv, tot, gg,
    att_o, gq_o, gk_o, gv_o, gs_o, gain_o,
    gs, gain, sem,
):
    copies = []

    def store(src, dst):
        copy = pltpu.make_async_copy(src, dst, sem.at[len(copies)])
        copy.start()
        copies.append(copy)

    store(att, att_o)
    store(gq, gq_o)
    store(gk, gk_o)
    store(gv, gv_o)
    gs[...] = tot[...].astype(F32)
    store(gs, gs_o)
    for h in range(HEADS):
        gain[:, h * D:(h + 1) * D] = gg[h:h + 1]
    store(gain, gain_o)
    for copy in copies:
        copy.wait()


def on_device(queries, key_rows, values, cotangent, carried_state, norm_gain):
    any_spec = pl.BlockSpec(memory_space=pl.ANY)
    vmem_spec = pl.BlockSpec(memory_space=pltpu.VMEM)
    wide = (L, WIDTH)
    slices = (ROW, HALF, D)
    sds = jax.ShapeDtypeStruct
    vmem = pltpu.VMEM
    held = (
        vmem(wide, BF16), vmem(wide, BF16), vmem(wide, BF16), vmem(wide, BF16),
        vmem(slices, BF16), vmem((TILE, D), F32),
    )
    parts = pl.pallas_call(
        comm_kernel,
        out_shape=held,
        in_specs=[pl.BlockSpec(memory_space=pltpu.HBM)] * 6,
        out_specs=[vmem_spec] * 6,
        scratch_shapes=[
            *[vmem(wide, BF16)] * 4, vmem((HALF, D), F32), vmem((1, WIDTH), F32),
            *[vmem(slices, BF16)] * 5,
            *[vmem(slices, BF16)] * 5,
            vmem((NZ, TILE, D), F32), vmem((ROW, TILE, D), F32), vmem((COL, TILE, D), F32),
            vmem((HEADS, L, L), BF16), vmem((HEADS, L, D), F32), vmem((HEADS, L, D), BF16),
            vmem(wide, F32), vmem(wide, F32),
            pltpu.SemaphoreType.DMA((6,)),
            pltpu.SemaphoreType.DMA((7, CHUNKS, 8)), pltpu.SemaphoreType.DMA((7, CHUNKS, 8)),
            pltpu.SemaphoreType.DMA((3, 8)), pltpu.SemaphoreType.DMA((3, 8)),
        ],
        compiler_params=pltpu.CompilerParams(
            collective_id=0, has_side_effects=True, vmem_limit_bytes=16 * 2**20
        ),
        name="scan_comm",
    )(*[pltpu.with_memory_space_constraint(x, pltpu.HBM) for x in (queries, key_rows, values, cotangent, carried_state.reshape(slices), norm_gain.reshape(1, WIDTH))])
    att, gq, gk, gv, gs, gain = pl.pallas_call(
        tail_kernel,
        out_shape=(
            sds(wide, BF16), sds(wide, BF16), sds(wide, BF16), sds(wide, BF16),
            sds(slices, F32), sds((1, WIDTH), F32),
        ),
        in_specs=[vmem_spec] * 6,
        out_specs=[any_spec] * 6,
        scratch_shapes=[
            vmem(slices, F32), vmem((1, WIDTH), F32),
            pltpu.SemaphoreType.DMA((6,)),
        ],
        compiler_params=pltpu.CompilerParams(vmem_limit_bytes=16 * 2**20),
        name="tail",
    )(*parts)
    return att, gq, gk, gv, gs.reshape(HEADS, D, D), gain.reshape(WIDTH)


def solution(mesh):
    in_specs = (
        P("seq", "head"),
        P("seq", "head"),
        P("seq", "head"),
        P("seq", "head"),
        P("head", None, None),
        P("head"),
    )
    out_specs = (
        P("seq", "head"),
        P("seq", "head"),
        P("seq", "head"),
        P("seq", "head"),
        P("head", None, None),
        P("head"),
    )
    return jax.shard_map(
        on_device, mesh=mesh, in_specs=in_specs, out_specs=out_specs, check_vma=False
    )
```

```python
import jax
import jax.numpy as jnp
from jax import lax
from jax.experimental import pallas as pl
from jax.experimental.pallas import tpu as pltpu
from jax.sharding import PartitionSpec as P

EPS = 1e-05
MESH = pl.DeviceIdType.MESH
F32 = jnp.float32
BF16 = jnp.bfloat16
ROW = 8
COL = 8
NZ = 8
HEADS = 4
D = 128
L = 256
WIDTH = HEADS * D
TOTAL_WIDTH = WIDTH * NZ
HALF = D // 2
TILE = 4
CHUNKS = 1
PIECE = HALF // CHUNKS
FAR_FIRST = (4, 5, 3, 6, 2, 7, 1)


def nn(a, b):
    return lax.dot_general(a, b, (((1,), (0,)), ((), ())), preferred_element_type=F32)


def nt(a, b):
    return lax.dot_general(a, b, (((1,), (1,)), ((), ())), preferred_element_type=F32)


def tn(a, b):
    return lax.dot_general(a, b, (((0,), (0,)), ((), ())), preferred_element_type=F32)


def comm_kernel(
    q_hbm, k_hbm, v_hbm, c_hbm, carry_hbm, gain_hbm,
    att, gq, gk, gv, tot, gg,
    q, k, v, c, carry, gain,
    sb, rb, cb, ps, pre,
    sb2, rb2, cb2, ps2, suf,
    zb, grow, gcol,
    sc_t, un, gu, gkp, gvp,
    in_sem, send_sem, recv_sem, tile_send, tile_recv,
):
    seq = lax.axis_index("seq")
    z = lax.axis_index("head")
    y = seq // ROW
    me = seq % ROW
    base = y * ROW

    def row_dev(kk):
        return (base + lax.rem(me + kk, ROW), z)

    def col_dev(kk):
        return (lax.rem(y + kk, COL) * ROW + me, z)

    def z_dev(kk):
        return (seq, lax.rem(z + kk, NZ))

    loads = []
    for i, (src, dst) in enumerate(
        ((k_hbm, k), (v_hbm, v), (q_hbm, q), (c_hbm, c), (carry_hbm.at[me], carry), (gain_hbm, gain))
    ):
        load = pltpu.make_async_copy(src, dst, in_sem.at[i])
        load.start()
        loads.append(load)

    barrier = pltpu.get_barrier_semaphore()
    for dev, count in ((row_dev, ROW), (col_dev, COL), (z_dev, NZ)):
        for kk in range(1, count):
            pl.semaphore_signal(barrier, inc=1, device_id=dev(kk), device_id_type=MESH)

    pending = []

    def exchange(sends, recvs, dev, count, src_of, dst_of, mine):
        for kk in FAR_FIRST:
            copy = pltpu.make_async_remote_copy(
                src_ref=src_of(lax.rem(mine + kk, count)),
                dst_ref=dst_of(mine),
                send_sem=sends.at[kk],
                recv_sem=recvs.at[kk],
                device_id=dev(kk),
                device_id_type=MESH,
            )
            copy.start()
            pending.append(copy)

        def wait():
            for kk in FAR_FIRST[::-1]:
                origin = lax.rem(mine + count - kk, count)
                pltpu.make_async_remote_copy(
                    src_ref=src_of(origin),
                    dst_ref=dst_of(origin),
                    send_sem=sends.at[kk],
                    recv_sem=recvs.at[kk],
                    device_id=dev(kk),
                    device_id_type=MESH,
                ).wait_recv()

        return wait

    def strip(n):
        return slice(n * PIECE, (n + 1) * PIECE)

    def piece(ref, i, n):
        return ref.at[i, pl.ds(n * PIECE, PIECE)]

    def scatter(stage, n, dev, count, src, dst, mine):
        return exchange(
            send_sem.at[stage, n], recv_sem.at[stage, n], dev, count,
            lambda t: piece(src, t, n), lambda t: piece(dst, t, n), mine,
        )

    def spread(stage, n, dev, count, ref, mine):
        return exchange(
            send_sem.at[stage, n], recv_sem.at[stage, n], dev, count,
            lambda t: piece(ref, mine, n), lambda t: piece(ref, t, n), mine,
        )

    def tiles(stage, dev, count, ref, mine):
        return exchange(
            tile_send.at[stage], tile_recv.at[stage], dev, count,
            lambda t: ref.at[mine], lambda t: ref.at[t], mine,
        )

    def head(ref, h):
        return ref[:, h * D:(h + 1) * D]

    rows = lax.broadcasted_iota(jnp.int32, (L, L), 0)
    cols = lax.broadcasted_iota(jnp.int32, (L, L), 1)
    lower = rows >= cols
    upper = rows <= cols

    loads[0].wait()
    loads[1].wait()
    for h in range(HEADS):
        state = tn(head(k, h), head(v, h)).astype(BF16)
        sb[2 * h] = state[:HALF]
        sb[2 * h + 1] = state[HALF:]
    pl.semaphore_wait(barrier, ROW + COL + NZ - 3)
    waits_a = [scatter(0, n, row_dev, ROW, sb, rb, me) for n in range(CHUNKS)]
    rb[me] = sb[me]

    loads[2].wait()
    for h in range(HEADS):
        score = jnp.where(lower, nt(head(q, h), head(k, h)), 0.0).astype(BF16)
        un[h] = nn(score, head(v, h))

    waits_b = []
    for n in range(CHUNKS):
        waits_a[n]()
        acc = rb[0, strip(n)].astype(F32)
        for r in range(1, ROW):
            acc = acc + rb[r, strip(n)].astype(F32)
        cb[y, strip(n)] = acc.astype(BF16)
        waits_b.append(spread(1, n, col_dev, COL, cb, y))

    for h in range(HEADS):
        sc_t[h] = jnp.where(upper, nt(head(k, h), head(q, h)), 0.0).astype(BF16)
    loads[3].wait()
    loads[4].wait()
    loads[5].wait()

    waits_c = []
    for n in range(CHUNKS):
        waits_b[n]()
        acc = carry[strip(n)]
        for r in range(COL):
            acc = acc + jnp.where(r < y, cb[r, strip(n)].astype(F32), 0.0)
        for r in range(ROW):
            ps[r, strip(n)] = acc.astype(BF16)
            if r < ROW - 1:
                acc = acc + rb[r, strip(n)].astype(F32)
        waits_c.append(scatter(2, n, row_dev, ROW, ps, pre, me))
    pre[me] = ps[me]
    for wait in waits_c:
        wait()

    square = jnp.zeros((L, D), F32)
    dots = jnp.zeros((L, D), F32)
    for h in range(HEADS):
        u = un[h] + nn(head(q, h), pre[2 * h:2 * h + 2].reshape(D, D))
        un[h] = u
        square = square + u * u
        dots = dots + head(c, h).astype(F32) * head(gain, h) * u

    def lane_sum(x):
        return jnp.sum(x.T, axis=0, keepdims=True)

    tile_row = lax.broadcasted_iota(jnp.int32, (TILE, D), 0)
    parts = (lane_sum(square[:D]), lane_sum(square[D:]), lane_sum(dots[:D]), lane_sum(dots[D:]))
    tile = jnp.zeros((TILE, D), F32)
    for i, part in enumerate(parts):
        tile = jnp.where(tile_row == i, part, tile)
    zb[z] = tile
    tiles(0, z_dev, NZ, zb, z)()
    sums = zb[0]
    for i in range(1, NZ):
        sums = sums + zb[i]
    mean = sums[0:2] / TOTAL_WIDTH + EPS
    inverse = 1.0 / jnp.sqrt(mean)
    factor = sums[2:4] / (TOTAL_WIDTH * mean)
    both = jnp.concatenate([inverse, factor, jnp.zeros((4, D), F32)], axis=0).T
    inv_col = jnp.concatenate([both[:, 0:1], both[:, 1:2]], axis=0)
    fac_col = jnp.concatenate([both[:, 2:3], both[:, 3:4]], axis=0)
    inv_col = jnp.broadcast_to(inv_col, (L, D))
    fac_col = jnp.broadcast_to(fac_col, (L, D))

    grow[me] = jnp.zeros((TILE, D), F32)
    for h in range(HEADS):
        cot = head(c, h).astype(F32)
        g = ((cot * head(gain, h) - un[h] * fac_col) * inv_col).astype(BF16)
        gu[h] = g
        state = tn(head(q, h), g).astype(BF16)
        sb2[2 * h] = state[:HALF]
        sb2[2 * h + 1] = state[HALF:]
    waits_a = [scatter(3, n, row_dev, ROW, sb2, rb2, me) for n in range(CHUNKS)]
    rb2[me] = sb2[me]

    for h in range(HEADS):
        normed = un[h] * inv_col
        att[:, h * D:(h + 1) * D] = (normed * head(gain, h)).astype(BF16)
        grow[me, h:h + 1] = jnp.sum(head(c, h).astype(F32) * normed, axis=0, keepdims=True)
    wait_g = tiles(1, row_dev, ROW, grow, me)

    waits_b = []
    for n in range(CHUNKS):
        waits_a[n]()
        acc = rb2[0, strip(n)].astype(F32)
        for r in range(1, ROW):
            acc = acc + rb2[r, strip(n)].astype(F32)
        cb2[y, strip(n)] = acc.astype(BF16)
        waits_b.append(spread(4, n, col_dev, COL, cb2, y))
    wait_g()
    gsum = grow[0]
    for r in range(1, ROW):
        gsum = gsum + grow[r]
    gcol[y] = gsum
    wait_g = tiles(2, col_dev, COL, gcol, y)

    for h in range(HEADS):
        lanes = slice(h * D, (h + 1) * D)
        mixed = jnp.where(lower, nt(gu[h], head(v, h)), 0.0).astype(BF16)
        gq[:, lanes] = (
            nn(mixed, head(k, h)) + nt(gu[h], pre[2 * h:2 * h + 2].reshape(D, D))
        ).astype(BF16)
        mixed_t = jnp.where(upper, nt(head(v, h), gu[h]), 0.0).astype(BF16)
        gkp[:, lanes] = nn(mixed_t, head(q, h))
        gvp[:, lanes] = nn(sc_t[h], gu[h])

    waits_c = []
    waits_t = []
    for n in range(CHUNKS):
        waits_b[n]()
        total = cb2[0, strip(n)].astype(F32)
        acc = jnp.zeros((PIECE, D), F32)
        for r in range(COL):
            row_sum = cb2[r, strip(n)].astype(F32)
            if r:
                total = total + row_sum
            acc = acc + jnp.where(r > y, row_sum, 0.0)
        for r in range(ROW - 1, -1, -1):
            ps2[r, strip(n)] = acc.astype(BF16)
            if r:
                acc = acc + rb2[r, strip(n)].astype(F32)
        waits_c.append(scatter(5, n, row_dev, ROW, ps2, suf, me))
        tot[me, strip(n)] = total.astype(BF16)
        waits_t.append(spread(6, n, row_dev, ROW, tot, me))
    suf[me] = ps2[me]
    wait_g()
    gsum = gcol[0]
    for r in range(1, COL):
        gsum = gsum + gcol[r]
    gg[...] = gsum
    for wait in waits_c:
        wait()
    for h in range(HEADS):
        lanes = slice(h * D, (h + 1) * D)
        suffix = suf[2 * h:2 * h + 2].reshape(D, D)
        gk[:, lanes] = (gkp[:, lanes] + nt(head(v, h), suffix)).astype(BF16)
        gv[:, lanes] = (gvp[:, lanes] + nn(head(k, h), suffix)).astype(BF16)
    for wait in waits_t:
        wait()
    for copy in pending:
        copy.wait_send()


def tail_kernel(
    att, gq, gk, gv, tot, gg,
    att_o, gq_o, gk_o, gv_o, gs_o, gain_o,
    gs, gain, sem,
):
    copies = []

    def store(src, dst):
        copy = pltpu.make_async_copy(src, dst, sem.at[len(copies)])
        copy.start()
        copies.append(copy)

    store(att, att_o)
    store(gq, gq_o)
    store(gk, gk_o)
    store(gv, gv_o)
    gs[...] = tot[...].astype(F32)
    store(gs, gs_o)
    for h in range(HEADS):
        gain[:, h * D:(h + 1) * D] = gg[h:h + 1]
    store(gain, gain_o)
    for copy in copies:
        copy.wait()


def on_device(queries, key_rows, values, cotangent, carried_state, norm_gain):
    any_spec = pl.BlockSpec(memory_space=pl.ANY)
    vmem_spec = pl.BlockSpec(memory_space=pltpu.VMEM)
    wide = (L, WIDTH)
    slices = (ROW, HALF, D)
    sds = jax.ShapeDtypeStruct
    vmem = pltpu.VMEM
    held = (
        vmem(wide, BF16), vmem(wide, BF16), vmem(wide, BF16), vmem(wide, BF16),
        vmem(slices, BF16), vmem((TILE, D), F32),
    )
    parts = pl.pallas_call(
        comm_kernel,
        out_shape=held,
        in_specs=[pl.BlockSpec(memory_space=pltpu.HBM)] * 6,
        out_specs=[vmem_spec] * 6,
        scratch_shapes=[
            *[vmem(wide, BF16)] * 4, vmem((HALF, D), F32), vmem((1, WIDTH), F32),
            *[vmem(slices, BF16)] * 5,
            *[vmem(slices, BF16)] * 5,
            vmem((NZ, TILE, D), F32), vmem((ROW, TILE, D), F32), vmem((COL, TILE, D), F32),
            vmem((HEADS, L, L), BF16), vmem((HEADS, L, D), F32), vmem((HEADS, L, D), BF16),
            vmem(wide, F32), vmem(wide, F32),
            pltpu.SemaphoreType.DMA((6,)),
            pltpu.SemaphoreType.DMA((7, CHUNKS, 8)), pltpu.SemaphoreType.DMA((7, CHUNKS, 8)),
            pltpu.SemaphoreType.DMA((3, 8)), pltpu.SemaphoreType.DMA((3, 8)),
        ],
        compiler_params=pltpu.CompilerParams(
            collective_id=0, has_side_effects=True, vmem_limit_bytes=16 * 2**20
        ),
        name="scan_comm",
    )(*[pltpu.with_memory_space_constraint(x, pltpu.HBM) for x in (queries, key_rows, values, cotangent, carried_state.reshape(slices), norm_gain.reshape(1, WIDTH))])
    att, gq, gk, gv, gs, gain = pl.pallas_call(
        tail_kernel,
        out_shape=(
            sds(wide, BF16), sds(wide, BF16), sds(wide, BF16), sds(wide, BF16),
            sds(slices, F32), sds((1, WIDTH), F32),
        ),
        in_specs=[vmem_spec] * 6,
        out_specs=[any_spec] * 6,
        scratch_shapes=[
            vmem(slices, F32), vmem((1, WIDTH), F32),
            pltpu.SemaphoreType.DMA((6,)),
        ],
        compiler_params=pltpu.CompilerParams(vmem_limit_bytes=16 * 2**20),
        name="tail",
    )(*parts)
    return att, gq, gk, gv, gs.reshape(HEADS, D, D), gain.reshape(WIDTH)


def solution(mesh):
    in_specs = (
        P("seq", "head"),
        P("seq", "head"),
        P("seq", "head"),
        P("seq", "head"),
        P("head", None, None),
        P("head"),
    )
    out_specs = (
        P("seq", "head"),
        P("seq", "head"),
        P("seq", "head"),
        P("seq", "head"),
        P("head", None, None),
        P("head"),
    )
    return jax.shard_map(
        on_device, mesh=mesh, in_specs=in_specs, out_specs=out_specs, check_vma=False
    )
```
